1024 devices in a mesh: dp: 128 (over y, z_lo, x), seq: 8 (over z_hi, core).
Axes of the slice: x: 8, y: 8, z: 8 (z_hi: 4, z_lo: 2; z = z_hi * 2 + z_lo), core: 2. Of those that a mesh axis runs over, the one named last changes fastest.
Arguments:
- cotangent: bfloat16 [128, 1024, 2048], P('dp', 'seq'), may hold values from -0.875 to 0.875
- expert_ids: int32 [128, 1024, 2], P('dp', 'seq'), may hold values from 0 to 15, as said below
- gate_probs: float32 [128, 1024, 2], P('dp', 'seq'), may hold values from 0.05 to 1
- hidden_acts: bfloat16 [7168, 16384], P('seq', 'dp'), may hold values from -6 to 6
- step_input: bfloat16 [128, 1024, 256], P('dp', 'seq'), may hold values from -6 to 6
- step_proj: bfloat16 [256, 4096], replicated, may hold values from -0.375 to 0.375
- step_bias: float32 [4096], replicated, may hold values from -1 to 1
- decay_rate: float32 [16, 4096], replicated, may hold values from 0.00048828125 to 0.05
- input_coef: float32 [128, 16, 1024], P('dp', None, 'seq'), may hold values from -4 to 4
- output_coef: float32 [128, 16, 1024], P('dp', None, 'seq'), may hold values from -0.5 to 0.5
- grad_output: bfloat16 [128, 1024, 4096], P('dp', 'seq'), may hold values from -6 to 6
- skip_weight: float32 [4096], replicated, may hold values from 0.5 to 1.5
Outputs:
- grad_down: float32 [2048, 7168], P('dp', 'seq')
- grad_x: bfloat16 [128, 1024, 4096], P('dp', 'seq')
The draws below stay inside these ranges and needn't reach their ends.
Inputs may be any that keep to these rules, and one draw needn't show every extreme that they name: `expert_ids`: each token names 2 different experts; among the tokens of one device (aligned blocks of 128 tokens of a sequence) every expert is named by exactly 16 of the pairs.
All inputs are finite; a program needn't handle non-finite values.
Results may differ from the reference program's by a relative error of at most 0.0029.
Values may be sent and summed in bfloat16 or wider, within the bound.
A program may use at most 64 MiB of HBM per device.

```python
import math
import jax
import jax.numpy as jnp
from jax import lax

D = 2048
TOP = 2
EXPERTS = 16
HIDDEN_SIZE = 7168
CH = 4096
STATE = 16
DT_RANK = 256
TOK_DEV = 128
CAP = 16
ROWS = 128
LENGTH = 1024
SEQS = 128
N_SEQ = 8


def draw_expert_ids(key, part):
    block_count = SEQS * (LENGTH // TOK_DEV)
    per_group = TOK_DEV // EXPERTS

    def one_block(position):
        token_key = jax.random.fold_in(key, 2 * position)
        cycle_key = jax.random.fold_in(key, 2 * position + 1)
        shuffled = jax.random.permutation(token_key, TOK_DEV)
        primary = jnp.zeros((TOK_DEV,), jnp.int32).at[shuffled].set(jnp.arange(TOK_DEV, dtype=jnp.int32) // per_group)
        labels = jax.random.permutation(cycle_key, EXPERTS).astype(jnp.int32)
        successor = jnp.zeros((EXPERTS,), jnp.int32).at[labels].set(jnp.roll(labels, -1))
        secondary = successor[primary]
        return jnp.stack([primary, secondary], axis=-1)
    blocks = jax.vmap(one_block)(jnp.arange(block_count, dtype=jnp.int32))
    return blocks.reshape(SEQS, LENGTH, TOP).astype(jnp.int32)


def strengthened(drawn, own_key, source, target, shards_of, factor):
    owner, partner = [(jnp.arange(drawn.shape[dim]) // (drawn.shape[dim] // shards_of)).reshape([-1 if axis == dim else 1 for axis in range(drawn.ndim)]) for dim in (source, target)]
    chosen = jax.random.permutation(own_key, shards_of)[partner]
    strong = (owner == chosen) | (owner == (partner + shards_of // 2) % shards_of)
    return jnp.where(strong, factor * drawn, drawn)


def block_scale(key, shape, split, least, high):
    level = 1.0
    for axis_at, blocks in split:
        draws = jax.random.uniform(jax.random.fold_in(jax.random.fold_in(key, 6), axis_at), (blocks,), jnp.float32, least / len(split), high / len(split))
        level = level * jnp.repeat(jnp.exp(draws), shape[axis_at] // blocks).reshape((-1,) + (1,) * (len(shape) - 1 - axis_at))
    return level


def normal_values(key, shape, scale, bound, split=(), held_as=jnp.bfloat16):
    array = scale * jax.random.normal(key, shape, jnp.float32)
    if split:
        array = array * block_scale(key, shape, split, -0.22, 0.18)
    return jnp.clip(array, -bound, bound).astype(held_as)


def heavy_noise(key, dims, scale, limit, cuts, heavy, kind=jnp.bfloat16):
    drawn = scale * jax.random.normal(key, dims, jnp.float32)
    if cuts:
        drawn = drawn * block_scale(key, dims, cuts, -0.22, 0.18)
    return jnp.clip(strengthened(drawn, jax.random.fold_in(key, 3), *heavy), -limit, limit).astype(kind)


def setup_inputs(seed: int = 0) -> dict:
    keys = jax.random.split(jax.random.key(seed), 13)
    return {
        "cotangent": heavy_noise(keys[0], (SEQS, LENGTH, D), (2.0 / (SEQS * ROWS) ** 0.5), 0.875, ((0, 128), (1, 8)), (0, 2, 128, 5.5)),
        "expert_ids": draw_expert_ids(jax.random.fold_in(keys[12], 71), 0),
        "gate_probs": jnp.clip(0.05 + 0.95 * jax.random.uniform(keys[2], (SEQS, LENGTH, TOP), jnp.float32) ** block_scale(keys[2], (SEQS, LENGTH, TOP), ((0, 128), (1, 8)), -0.2, 0.2), 0.05, 1.0),
        "hidden_acts": normal_values(keys[3], (HIDDEN_SIZE, SEQS * ROWS), 1.0, 6.0, ((0, 8), (1, 128))),
        "step_input": normal_values(keys[4], (SEQS, LENGTH, DT_RANK), 1.0, 6.0, ((0, 128), (1, 8))),
        "step_proj": normal_values(keys[5], (DT_RANK, CH), DT_RANK ** -0.5, 0.375),
        "step_bias": jnp.clip(jax.random.uniform(keys[6], (CH,), jnp.float32, -1.0, 1.0), -1.0, 1.0),
        "decay_rate": jnp.clip(jnp.exp(jax.random.uniform(keys[7], (STATE, CH), jnp.float32, math.log(0.00048828125), math.log(0.05))), 0.00048828125, 0.05),
        "input_coef": normal_values(keys[8], (SEQS, STATE, LENGTH), 0.25, 4.0, ((0, 128), (2, 8)), jnp.float32),
        "output_coef": normal_values(keys[9], (SEQS, STATE, LENGTH), (1.0 / LENGTH ** 0.5), 0.5, ((0, 128), (2, 8)), jnp.float32),
        "grad_output": normal_values(keys[10], (SEQS, LENGTH, CH), 1.0, 6.0, ((0, 128), (1, 8))),
        "skip_weight": jnp.clip(jax.random.uniform(keys[11], (CH,), jnp.float32, 0.5, 1.5), 0.5, 1.5),
    }


def reference(cotangent, expert_ids, gate_probs, hidden_acts, step_input, step_proj, step_bias, decay_rate, input_coef, output_coef, grad_output, skip_weight):
    pair_count = TOK_DEV * TOP
    block_total = SEQS * N_SEQ
    chosen = (expert_ids.reshape(block_total, pair_count) == 0).astype(jnp.int32)
    before = jnp.cumsum(chosen, axis=1) - chosen
    destination = jnp.where(chosen == 1, before, CAP).astype(jnp.int32)
    block_index = jnp.broadcast_to(jnp.arange(block_total, dtype=jnp.int32)[:, None], (block_total, pair_count))
    pair_token = jnp.broadcast_to((jnp.arange(pair_count, dtype=jnp.int32) // TOP)[None, :], (block_total, pair_count))
    token_of_slot = jnp.zeros((block_total, CAP + 1), jnp.int32).at[block_index, destination].set(pair_token)[:, :CAP]
    gate_of_slot = jnp.zeros((block_total, CAP + 1), gate_probs.dtype).at[block_index, destination].set(gate_probs.reshape(block_total, pair_count))[:, :CAP]
    cot_blocks = cotangent.reshape(block_total, TOK_DEV, D)
    picked = jnp.take_along_axis(cot_blocks, token_of_slot[:, :, None], axis=1)
    routed = (picked.astype(jnp.float32) * gate_of_slot[:, :, None]).astype(jnp.bfloat16).reshape(SEQS * ROWS, D)
    grad_down = jnp.transpose(jnp.dot(hidden_acts.astype(jnp.float32), routed.astype(jnp.float32), precision=lax.Precision.HIGHEST, preferred_element_type=jnp.float32))

    negative_rate = -decay_rate
    proj_wide = step_proj.astype(jnp.float32)

    def token_step(state_carry, inputs):
        step_rows, grad_rows, in_cols, out_cols = inputs
        step_size = jax.nn.softplus(jnp.dot(step_rows.astype(jnp.float32), proj_wide, precision=lax.Precision.HIGHEST, preferred_element_type=jnp.float32) + step_bias[None, :])
        out_grad = grad_rows.astype(jnp.float32)
        adjoint = out_cols[:, :, None] * out_grad[:, None, :] + state_carry
        result = step_size * jnp.sum(in_cols[:, :, None] * adjoint, axis=1) + skip_weight[None, :] * out_grad
        passed = jnp.exp(step_size[:, None, :] * negative_rate[None, :, :]) * adjoint
        return passed, result.astype(jnp.bfloat16)

    inputs = (jnp.moveaxis(step_input, 1, 0), jnp.moveaxis(grad_output, 1, 0), jnp.moveaxis(input_coef, 2, 0), jnp.moveaxis(output_coef, 2, 0))
    final_state, token_rows = lax.scan(token_step, jnp.zeros((SEQS, STATE, CH), jnp.float32), inputs, reverse=True)
    grad_x = jnp.moveaxis(token_rows, 0, 1)
    return (grad_down, grad_x)
```

```python
import functools
import math

import jax
import jax.numpy as jnp
from jax import lax
from jax.experimental import pallas as pl
from jax.experimental.pallas import tpu as pltpu
from jax.sharding import PartitionSpec as P

MESH = pl.DeviceIdType.MESH
LANES = 128
TILE = 8 * LANES
LOG2E = math.log2(math.e)
UNROLL = 8
X_SIZE = 8
Y_SIZE = 8
PEERS = 8
SLOTS = 16
VMEM_LIMIT = 40 << 20


def softplus(v):
    return jnp.maximum(v, 0.0) + jnp.log1p(jnp.exp(-jnp.abs(v)))


def route(ids_ref, gate_ref, cot_ref, routed_ref):
    tokens = cot_ref.shape[0]
    named = (ids_ref[...] == 0).astype(jnp.float32)
    chosen = jnp.sum(named, axis=1, keepdims=True)
    gate = jnp.sum(named * gate_ref[...], axis=1, keepdims=True)
    row = lax.broadcasted_iota(jnp.int32, (tokens, tokens), 0)
    col = lax.broadcasted_iota(jnp.int32, (tokens, tokens), 1)
    earlier = jnp.where(col < row, 1.0, 0.0).astype(jnp.bfloat16)
    spread = jnp.broadcast_to(chosen, (tokens, LANES))
    rank = jnp.dot(earlier, spread.astype(jnp.bfloat16), preferred_element_type=jnp.float32)
    lane = lax.broadcasted_iota(jnp.int32, (tokens, LANES), 1).astype(jnp.float32)
    pick = jnp.where(rank == lane, spread, 0.0)[:, :SLOTS].astype(jnp.bfloat16)
    scaled = (cot_ref[...].astype(jnp.float32) * gate).astype(jnp.bfloat16)
    routed = lax.dot_general(
        pick, scaled, (((0,), (0,)), ((), ())), preferred_element_type=jnp.float32
    ).astype(jnp.bfloat16)
    width = routed_ref.shape[2]
    for y in range(routed_ref.shape[0]):
        routed_ref[y] = routed[:, y * width : (y + 1) * width]


def first_kernel(
    out_coef, ids_ref, gate_ref, cot_ref, x_ref, w_ref, b_ref, d_ref, g_ref,
    routed_ref, step_ref, message_ref, rate_ref, grads, state,
):
    tokens, states, tiles = x_ref.shape[0], d_ref.shape[0], TILE // LANES

    @pl.when(pl.program_id(0) == 0)
    def _():
        route(ids_ref, gate_ref, cot_ref, routed_ref)

    step = softplus(
        jnp.dot(x_ref[...], w_ref[...], preferred_element_type=jnp.float32) + b_ref[...]
    )
    g = g_ref[...].astype(jnp.float32)
    d = d_ref[...] * (-LOG2E)
    for k in range(tiles):
        lanes = slice(k * LANES, (k + 1) * LANES)
        step_ref[k * tokens : (k + 1) * tokens, :] = step[:, lanes]
        grads[k * tokens : (k + 1) * tokens, :] = g[:, lanes]
        rate_ref[k * states : (k + 1) * states, :] = d[:, lanes]
    rate = [rate_ref[pl.ds(n, tiles, stride=states), :] for n in range(states)]

    def body(i, carry):
        total, held = carry
        t = tokens - 1 - i
        s = step_ref[pl.ds(t, tiles, stride=tokens), :]
        grad = grads[pl.ds(t, tiles, stride=tokens), :]
        held = tuple(
            jnp.exp2(s * rate[n]) * (out_coef[n, t] * grad + held[n]) for n in range(states)
        )
        return total + s, held

    zero = jnp.zeros((tiles, LANES), jnp.float32)
    total, held = lax.fori_loop(0, tokens, body, (zero, (zero,) * states), unroll=UNROLL)
    for n in range(states):
        state[pl.ds(n, tiles, stride=states), :] = held[n]
    half, rows = tiles // 2, tiles // 2 * states
    for part in range(2):
        message_ref[part, :rows, :] = state[part * rows : (part + 1) * rows, :]
        message_ref[part, rows : rows + tiles, :] = jnp.concatenate(
            [total[part * half : (part + 1) * half], zero[:half]], axis=0
        )


def first(out_coef, ids, gate, cot, x, w, b, d, g):
    tokens, inner = x.shape
    channels, states, width = w.shape[1], d.shape[0], cot.shape[1]
    steps, tiles = channels // TILE, TILE // LANES
    whole = lambda *shape: pl.BlockSpec(shape, lambda q: (0,) * len(shape))
    message = (2, tiles // 2 * states + tiles, LANES)
    return pl.pallas_call(
        first_kernel,
        grid=(steps,),
        in_specs=[
            pl.BlockSpec(memory_space=pltpu.SMEM),
            whole(*ids.shape),
            whole(*gate.shape),
            whole(*cot.shape),
            whole(tokens, inner),
            pl.BlockSpec((inner, TILE), lambda q: (0, q)),
            pl.BlockSpec((1, TILE), lambda q: (0, q)),
            pl.BlockSpec((states, TILE), lambda q: (0, q)),
            pl.BlockSpec((tokens, TILE), lambda q: (0, q)),
        ],
        out_specs=[
            whole(Y_SIZE, SLOTS, width // Y_SIZE),
            pl.BlockSpec((tiles * tokens, LANES), lambda q: (q, 0)),
            pl.BlockSpec(message, lambda q: (q, 0, 0)),
            pl.BlockSpec((tiles * states, LANES), lambda q: (q, 0)),
        ],
        out_shape=[
            jax.ShapeDtypeStruct((Y_SIZE, SLOTS, width // Y_SIZE), jnp.bfloat16),
            jax.ShapeDtypeStruct((steps * tiles * tokens, LANES), jnp.float32),
            jax.ShapeDtypeStruct((2 * steps,) + message[1:], jnp.float32),
            jax.ShapeDtypeStruct((steps * tiles * states, LANES), jnp.float32),
        ],
        scratch_shapes=[
            pltpu.VMEM((tiles * tokens, LANES), jnp.float32),
            pltpu.VMEM((tiles * states, LANES), jnp.float32),
        ],
        compiler_params=pltpu.CompilerParams(vmem_limit_bytes=VMEM_LIMIT),
        name="first",
    )(out_coef, ids, gate, cot, x, w, b, d, g)


def exchange_kernel(
    hidden_ref, routed_ref, message_ref, rate_ref, incoming_ref, down_ref,
    hidden, slices, rows, states, sums, arrived, partial, parts,
    hs, hr, ds, dr, zs, zr, fs, fr, ss, sr, ts, tr, ps, pr,
):
    i, j = lax.axis_index("dp"), lax.axis_index("seq")
    y, zx = i // 16, lax.rem(i, 16)
    zl, x = zx // 8, lax.rem(zx, 8)
    units = hidden_ref.shape[0]
    split = units // 2 // LANES * LANES + LANES
    chunks = ((0, split), (split, units - split))
    sibling = j + 1 - 2 * lax.rem(j, 2)

    def on_y(k):
        return {"dp": lax.rem(y + k, Y_SIZE) * 16 + zx, "seq": j}

    def on_seq(k):
        return {"dp": i, "seq": lax.rem(j + k, PEERS)}

    def on_plane(k):
        other = lax.rem(zl + k // 8, 2) * 8 + lax.rem(x + k % 8, 8)
        return other, {"dp": y * 16 + other, "seq": j}

    def copy(src, dst, send, recv, device):
        c = pltpu.make_async_remote_copy(
            src_ref=src, dst_ref=dst, send_sem=send, recv_sem=recv,
            device_id=device, device_id_type=MESH,
        )
        c.start()
        return c

    barrier = pltpu.get_barrier_semaphore()
    greeted = [on_y(k) for k in range(1, Y_SIZE)]
    greeted += [on_seq(k) for k in range(1, PEERS)]
    greeted += [on_plane(k)[1] for k in range(1, 16)]
    for device in greeted:
        pl.semaphore_signal(barrier, inc=1, device_id=device, device_id_type=MESH)
    pl.semaphore_wait(barrier, len(greeted))

    sliced = [
        copy(routed_ref.at[lax.rem(y + k, Y_SIZE)], slices.at[y], ds.at[k], dr.at[k], on_y(k))
        for k in range(1, Y_SIZE)
    ]
    told = [
        copy(message_ref.at[lax.rem(j + k, PEERS)], states.at[j], ss.at[k], sr.at[k], on_seq(k))
        for k in range(1, PEERS)
    ]
    gathered = {}

    def pass_on(hop, c):
        at, size = chunks[c]
        here = pl.ds(at, size)
        for way, last in ((0, 4), (1, 3)):
            if hop < last:
                slot = hop if way == 0 else (0 if hop == 0 else 4 + hop)
                land = hop + 1 if way == 0 else 5 + hop
                source = hidden_ref if hop == 0 else hidden.at[slot]
                gathered[hop, c, way] = copy(
                    source.at[here], hidden.at[land, here], hs.at[c, land], hr.at[c, land],
                    on_y(1 if way == 0 else Y_SIZE - 1),
                )

    def arrive(hop, c):
        for way in (0, 1):
            if (hop, c, way) in gathered:
                gathered[hop, c, way].wait_recv()

    for c in range(2):
        pass_on(0, c)
    slices[y] = routed_ref[y]
    states[j] = message_ref[j]

    for c in sliced:
        c.wait_recv()
    rows[:, j] = slices[...]
    spread = [
        copy(slices, rows.at[:, j], zs.at[k], zr.at[k], on_seq(2 * k)) for k in range(1, 4)
    ]
    spread.append(copy(slices, rows.at[:, j], zs.at[0], zr.at[0], {"dp": i, "seq": sibling}))
    for c in range(2):
        arrive(0, c)
        pass_on(1, c)

    for c in told:
        c.wait_recv()
    lines = rate_ref.shape[1]
    factor = rate_ref[j]
    block = lines // 4
    current = jnp.zeros((lines, LANES), jnp.float32)
    for b in reversed(range(PEERS)):
        sums[b] = current
        if b:
            total = jnp.concatenate(
                [
                    jnp.broadcast_to(states[b, lines + k : lines + k + 1, :], (block, LANES))
                    for k in range(4)
                ],
                axis=0,
            )
            current = states[b, :lines, :] + jnp.exp2(factor * total) * current
    returned = [
        copy(sums.at[lax.rem(j + k, PEERS)], arrived.at[j], ts.at[k], tr.at[k], on_seq(k))
        for k in range(1, PEERS)
    ]
    arrived[j] = sums[j]

    for c in range(2):
        arrive(1, c)
        pass_on(2, c)
    forwarded = []
    for k in range(1, 4):
        spread[k - 1].wait_recv()
        origin = lax.rem(j + PEERS - 2 * k, PEERS)
        forwarded.append(
            copy(rows.at[:, origin], rows.at[:, origin], fs.at[k], fr.at[k], {"dp": i, "seq": sibling})
        )
    for c in range(2):
        arrive(2, c)
        pass_on(3, c)
    spread[3].wait_recv()
    for c in forwarded:
        c.wait_recv()

    depth, width = rows.shape[1] * rows.shape[2], rows.shape[3]

    def term(slot, c):
        at, size = chunks[c]
        origin = lax.rem(y + Y_SIZE - slot, Y_SIZE) if slot <= 4 else lax.rem(y + slot - 4, Y_SIZE)
        left = rows[origin].reshape(depth, width)
        right = (hidden_ref if slot == 0 else hidden.at[slot])[pl.ds(at, size), :]
        return lax.dot_general(
            left, right, (((0,), (1,)), ((), ())), preferred_element_type=jnp.float32
        )

    early = []
    for c in range(2):
        total = term(0, c)
        for slot in (1, 2, 3, 5, 6, 7):
            total = total + term(slot, c)
        at, size = chunks[c]
        partial[:, :, at : at + size] = total.reshape(16, SLOTS, size)
    scattered = []
    for c in range(2):
        at, size = chunks[c]
        arrive(3, c)
        partial[:, :, at : at + size] += term(4, c).reshape(16, SLOTS, size)
        for k in range(1, 16):
            other, device = on_plane(k)
            scattered.append(
                copy(
                    partial.at[other, :, pl.ds(at, size)], parts.at[k, :, pl.ds(at, size)],
                    ps.at[c, k], pr.at[c, k], device,
                )
            )
    for c in returned:
        c.wait_recv()
    incoming_ref[...] = arrived[...]
    for c in range(2):
        at, size = chunks[c]
        total = partial[zx, :, at : at + size]
        for k in range(1, 16):
            scattered[c * 15 + k - 1].wait_recv()
            total = total + parts[k, :, at : at + size]
        down_ref[:, at : at + size] = total
    for c in sliced + told + list(gathered.values()) + spread + returned + forwarded + scattered:
        c.wait_send()


def exchange(hidden, routed, message, rate):
    units, depth = hidden.shape
    width = routed.shape[2]
    lines = rate.shape[1]
    vmem = pl.BlockSpec(memory_space=pltpu.VMEM)
    sem = pltpu.SemaphoreType.DMA
    return pl.pallas_call(
        exchange_kernel,
        in_specs=[vmem] * 4,
        out_specs=[vmem] * 2,
        out_shape=[
            jax.ShapeDtypeStruct((PEERS, lines, LANES), jnp.float32),
            jax.ShapeDtypeStruct((SLOTS, units), jnp.float32),
        ],
        scratch_shapes=[
            pltpu.VMEM((8, units, depth), jnp.bfloat16),
            pltpu.VMEM((Y_SIZE, SLOTS, width), jnp.bfloat16),
            pltpu.VMEM((Y_SIZE, PEERS, SLOTS, width), jnp.bfloat16),
            pltpu.VMEM(message.shape, jnp.float32),
            pltpu.VMEM((PEERS, lines, LANES), jnp.float32),
            pltpu.VMEM((PEERS, lines, LANES), jnp.float32),
            pltpu.VMEM((16, SLOTS, units), jnp.float32),
            pltpu.VMEM((16, SLOTS, units), jnp.float32),
            sem((2, 8)), sem((2, 8)),
            sem((8,)), sem((8,)),
            sem((4,)), sem((4,)),
            sem((4,)), sem((4,)),
            sem((8,)), sem((8,)),
            sem((8,)), sem((8,)),
            sem((2, 16)), sem((2, 16)),
        ],
        compiler_params=pltpu.CompilerParams(
            collective_id=0, has_side_effects=True, vmem_limit_bytes=VMEM_LIMIT
        ),
        name="exchange",
    )(hidden, routed, message, rate)


def last_kernel(
    out_coef, in_coef, step_ref, incoming_ref, rate_ref, g_ref, skip_ref, out_ref, grads, results
):
    tokens, tiles = g_ref.shape[0], TILE // LANES
    states = rate_ref.shape[0] // tiles
    g = g_ref[...].astype(jnp.float32)
    for k in range(tiles):
        grads[k * tokens : (k + 1) * tokens, :] = g[:, k * LANES : (k + 1) * LANES]
    rate = [rate_ref[pl.ds(n, tiles, stride=states), :] for n in range(states)]

    def body(i, held):
        t = tokens - 1 - i
        s = step_ref[pl.ds(t, tiles, stride=tokens), :]
        grad = grads[pl.ds(t, tiles, stride=tokens), :]
        after, sums = [], [None] * 4
        for n in range(states):
            adjoint = out_coef[n, t] * grad + held[n]
            product = in_coef[n, t] * adjoint
            sums[n % 4] = product if n < 4 else sums[n % 4] + product
            after.append(jnp.exp2(s * rate[n]) * adjoint)
        results[pl.ds(t, tiles, stride=tokens), :] = s * ((sums[0] + sums[1]) + (sums[2] + sums[3]))
        return tuple(after)

    held = tuple(incoming_ref[pl.ds(n, tiles, stride=states), :] for n in range(states))
    lax.fori_loop(0, tokens, body, held, unroll=UNROLL // 2)
    skip = skip_ref[...]
    for k in range(tiles):
        lanes = slice(k * LANES, (k + 1) * LANES)
        out_ref[:, lanes] = (
            results[k * tokens : (k + 1) * tokens, :] + skip[:, lanes] * g[:, lanes]
        ).astype(jnp.bfloat16)


def last(out_coef, in_coef, step, incoming, rate, g, skip):
    tokens, channels = g.shape
    steps, tiles = channels // TILE, TILE // LANES
    states = rate.shape[0] // (steps * tiles)
    return pl.pallas_call(
        last_kernel,
        grid=(steps,),
        in_specs=[
            pl.BlockSpec(memory_space=pltpu.SMEM),
            pl.BlockSpec(memory_space=pltpu.SMEM),
            pl.BlockSpec((tiles * tokens, LANES), lambda q: (q, 0)),
            pl.BlockSpec((tiles * states, LANES), lambda q: (q, 0)),
            pl.BlockSpec((tiles * states, LANES), lambda q: (q, 0)),
            pl.BlockSpec((tokens, TILE), lambda q: (0, q)),
            pl.BlockSpec((1, TILE), lambda q: (0, q)),
        ],
        out_specs=pl.BlockSpec((tokens, TILE), lambda q: (0, q)),
        out_shape=jax.ShapeDtypeStruct((tokens, channels), jnp.bfloat16),
        scratch_shapes=[
            pltpu.VMEM((tiles * tokens, LANES), jnp.float32),
            pltpu.VMEM((tiles * tokens, LANES), jnp.float32),
        ],
        compiler_params=pltpu.CompilerParams(vmem_limit_bytes=VMEM_LIMIT),
        name="last",
    )(out_coef, in_coef, step, incoming, rate, g, skip)


def on_device(
    cotangent, expert_ids, gate_probs, hidden_acts, step_input, step_proj, step_bias,
    decay_rate, input_coef, output_coef, grad_output, skip_weight,
):
    out_coef, in_coef, g = output_coef[0], input_coef[0], grad_output[0]
    routed, step, message, rate = first(
        out_coef, expert_ids[0], gate_probs[0], cotangent[0], step_input[0], step_proj,
        step_bias[None, :], decay_rate, g,
    )
    incoming, grad_down = exchange(hidden_acts, routed, message, rate.reshape(PEERS, -1, LANES))
    grad_x = last(
        out_coef, in_coef, step, incoming.reshape(-1, LANES), rate, g, skip_weight[None, :]
    )
    return (grad_down, grad_x[None])


def solution(mesh):
    return jax.shard_map(
        on_device,
        mesh=mesh,
        in_specs=(
            P("dp", "seq", None),
            P("dp", "seq", None),
            P("dp", "seq", None),
            P("seq", "dp"),
            P("dp", "seq", None),
            P(),
            P(),
            P(),
            P("dp", None, "seq"),
            P("dp", None, "seq"),
            P("dp", "seq", None),
            P(),
        ),
        out_specs=(P("dp", "seq"), P("dp", "seq", None)),
        check_vma=False,
    )
```

```python
import functools
import math

import jax
import jax.numpy as jnp
from jax import lax
from jax.experimental import pallas as pl
from jax.experimental.pallas import tpu as pltpu
from jax.sharding import PartitionSpec as P

MESH = pl.DeviceIdType.MESH
LANES = 128
TILE = 8 * LANES
LOG2E = math.log2(math.e)
UNROLL = 4
X_SIZE = 8
Y_SIZE = 8
PEERS = 8
SLOTS = 16
VMEM_LIMIT = 56 << 20


def softplus(v):
    return jnp.maximum(v, 0.0) + jnp.log1p(jnp.exp(-jnp.abs(v)))


def route(ids_ref, gate_ref, cot_ref, routed_ref):
    tokens = cot_ref.shape[0]
    named = (ids_ref[...] == 0).astype(jnp.float32)
    chosen = jnp.sum(named, axis=0, keepdims=True)
    gate = jnp.sum(named * gate_ref[...], axis=0, keepdims=True)
    row = lax.broadcasted_iota(jnp.int32, (tokens, tokens), 0)
    col = lax.broadcasted_iota(jnp.int32, (tokens, tokens), 1)
    earlier = jnp.where(row < col, 1.0, 0.0).astype(jnp.bfloat16)
    spread = jnp.broadcast_to(chosen, (SLOTS, tokens))
    rank = jnp.dot(spread.astype(jnp.bfloat16), earlier, preferred_element_type=jnp.float32)
    slot = lax.broadcasted_iota(jnp.int32, (SLOTS, tokens), 0).astype(jnp.float32)
    pick = jnp.where(rank == slot, spread, 0.0)
    weight = jnp.sum(pick * gate, axis=1, keepdims=True)
    width = routed_ref.shape[2]
    for y in range(routed_ref.shape[0]):
        picked = jnp.dot(
            pick.astype(jnp.bfloat16),
            cot_ref[:, y * width : (y + 1) * width],
            preferred_element_type=jnp.float32,
        )
        routed_ref[y] = (weight * picked).astype(jnp.bfloat16)


def fused_kernel(
    out_coef, in_coef, ids_hbm, gate_hbm, cot_hbm, hid_hbm, x_hbm, w_hbm, b_hbm, d_hbm, g_hbm, skip_hbm,
    down_hbm, gx_hbm,
    ids_ref, gate_ref, cot_ref, hid_ref, x_ref, w_ref, b_ref, d_ref, g_ref, skip_ref, down_ref, gx_ref,
    routed_ref, steps, grads, rates, message, told, sums, arrived, results,
    hidden, slices, rows, partial, rounded, parts,
    local, hs, hr, ds, dr, zs, zr, fs, fr, ss, sr, ts, tr, ps, pr,
):
    i, j = lax.axis_index("dp"), lax.axis_index("seq")
    y, zx = i // 16, lax.rem(i, 16)
    zl, x = zx // 8, lax.rem(zx, 8)
    units = hid_ref.shape[0]
    split = units // 2 // LANES * LANES + LANES
    chunks = ((0, split), (split, units - split))
    sibling = j + 1 - 2 * lax.rem(j, 2)
    tokens, states, tiles = x_ref.shape[0], d_ref.shape[0], TILE // LANES
    quarters = w_ref.shape[1] // TILE
    pairs = quarters // 2
    sent = told.shape[2]
    lines = 2 * states

    def fetch(k, src, dst):
        c = pltpu.make_async_copy(src, dst, local.at[k])
        c.start()
        return c

    def columns(q):
        return pl.ds(q * TILE, TILE)

    small = [
        fetch(0, ids_hbm, ids_ref), fetch(1, gate_hbm, gate_ref), fetch(2, cot_hbm, cot_ref),
        fetch(3, x_hbm, x_ref), fetch(4, b_hbm, b_ref), fetch(5, d_hbm, d_ref), fetch(6, skip_hbm, skip_ref),
    ]
    weights, outputs = [], []
    for q in range(quarters):
        weights.append(fetch(8 + q, w_hbm.at[:, columns(q)], w_ref.at[:, columns(q)]))
        outputs.append(fetch(12 + q, g_hbm.at[:, columns(q)], g_ref.at[:, columns(q)]))
    held_units = fetch(7, hid_hbm, hid_ref)

    def on_y(k):
        return {"dp": lax.rem(y + k, Y_SIZE) * 16 + zx, "seq": j}

    def on_seq(k):
        return {"dp": i, "seq": lax.rem(j + k, PEERS)}

    def on_plane(k):
        other = lax.rem(zl + k // 8, 2) * 8 + lax.rem(x + k % 8, 8)
        return other, {"dp": y * 16 + other, "seq": j}

    barrier = pltpu.get_barrier_semaphore()
    greeted = [on_y(k) for k in range(1, Y_SIZE)]
    greeted += [on_seq(k) for k in range(1, PEERS)]
    greeted += [on_plane(k)[1] for k in range(1, 16)]
    for device in greeted:
        pl.semaphore_signal(barrier, inc=1, device_id=device, device_id_type=MESH)

    started = []

    def copy(src, dst, send, recv, device):
        c = pltpu.make_async_remote_copy(
            src_ref=src, dst_ref=dst, send_sem=send, recv_sem=recv,
            device_id=device, device_id_type=MESH,
        )
        c.start()
        started.append(c)
        return c

    gathered = {}

    def pass_on(hop):
        for c in range(2):
            at, size = chunks[c]
            here = pl.ds(at, size)
            for way, final in ((0, 4), (1, 3)):
                if hop < final:
                    if hop:
                        gathered[hop - 1, c, way].wait_recv()
                    slot = hop if way == 0 else 4 + hop
                    land = hop + 1 if way == 0 else 5 + hop
                    source = hid_ref if hop == 0 else hidden.at[slot]
                    gathered[hop, c, way] = copy(
                        source.at[here], hidden.at[land, here], hs.at[c, land], hr.at[c, land],
                        on_y(1 if way == 0 else Y_SIZE - 1),
                    )

    def prepare(q):
        weights[q].wait()
        outputs[q].wait()
        own = slice(q * TILE, (q + 1) * TILE)
        step = softplus(
            jnp.dot(x_ref[...], w_ref[:, own], preferred_element_type=jnp.float32) + b_ref[:, own]
        )
        g = g_ref[:, own].astype(jnp.float32)
        d = d_ref[:, own] * (-LOG2E)
        for k in range(tiles):
            lanes = slice(k * LANES, (k + 1) * LANES)
            steps[q, k * tokens : (k + 1) * tokens, :] = step[:, lanes]
            grads[q, k * tokens : (k + 1) * tokens, :] = g[:, lanes]
            rates[q, k * states : (k + 1) * states, :] = d[:, lanes]

    def rate_of(q):
        return [rates[q, pl.ds(n, tiles, stride=states), :] for n in range(states)]

    def at_token(ref, q, t):
        return ref[q, pl.ds(t, tiles, stride=tokens), :]

    zero = jnp.zeros((tiles, LANES), jnp.float32)

    def scan_states(q, half, carry):
        rate = rate_of(q)
        count = tokens // 2

        def body(k, carry):
            total, held = carry
            t = tokens - 1 - half * count - k
            s, grad = at_token(steps, q, t), at_token(grads, q, t)
            held = tuple(
                jnp.exp2(s * rate[n]) * (out_coef[n, t] * grad + held[n]) for n in range(states)
            )
            return total + s, held

        return lax.fori_loop(0, count, body, carry, unroll=UNROLL)

    def finish_states(q, carry):
        total, held = carry
        for n in range(states):
            message[q // 2, pl.ds(q % 2 * states + n, tiles, stride=sent), :] = held[n]
        message[q // 2, pl.ds(lines + q % 2, tiles, stride=sent), :] = total

    def scan_states_whole(q):
        finish_states(q, scan_states(q, 1, scan_states(q, 0, (zero, (zero,) * states))))

    def tell(a):
        return [
            copy(
                message.at[a, pl.ds(pl.multiple_of(lax.rem(j + k, PEERS) * sent, 8), sent), :],
                told.at[a, j], ss.at[a, k], sr.at[a, k], on_seq(k),
            )
            for k in range(1, PEERS)
        ]

    def combine(a, incoming):
        told[a, j] = message[a, pl.ds(pl.multiple_of(j * sent, 8), sent), :]
        mine = pl.ds(pl.multiple_of(j * states, 8), states)
        factor = jnp.concatenate([rates[2 * a, mine, :], rates[2 * a + 1, mine, :]], axis=0)
        for c in incoming:
            c.wait_recv()
        current = jnp.zeros((lines, LANES), jnp.float32)
        for b in reversed(range(PEERS)):
            sums[a, b] = current
            if b:
                total = jnp.concatenate(
                    [
                        jnp.broadcast_to(told[a, b, lines + k : lines + k + 1, :], (states, LANES))
                        for k in range(2)
                    ],
                    axis=0,
                )
                current = told[a, b, :lines, :] + jnp.exp2(factor * total) * current
        slot = pl.ds(pl.multiple_of(j * lines, 8), lines)
        back = [
            copy(
                sums.at[a, lax.rem(j + k, PEERS)], arrived.at[a, slot, :], ts.at[a, k], tr.at[a, k], on_seq(k)
            )
            for k in range(1, PEERS)
        ]
        arrived[a, slot, :] = sums[a, j]
        return back

    def scan_outputs(q):
        rate = rate_of(q)

        def body(k, held):
            t = tokens - 1 - k
            s, grad = at_token(steps, q, t), at_token(grads, q, t)
            after, total = [], [None] * 4
            for n in range(states):
                adjoint = out_coef[n, t] * grad + held[n]
                product = in_coef[n, t] * adjoint
                total[n % 4] = product if n < 4 else total[n % 4] + product
                after.append(jnp.exp2(s * rate[n]) * adjoint)
            results[pl.ds(t, tiles, stride=tokens), :] = s * ((total[0] + total[1]) + (total[2] + total[3]))
            return tuple(after)

        held = tuple(
            arrived[q // 2, pl.ds(q % 2 * states + n, tiles, stride=lines), :] for n in range(states)
        )
        lax.fori_loop(0, tokens, body, held, unroll=UNROLL)
        for k in range(tiles):
            lanes = slice(q * TILE + k * LANES, q * TILE + (k + 1) * LANES)
            gx_ref[:, lanes] = (
                results[k * tokens : (k + 1) * tokens, :]
                + skip_ref[:, lanes] * g_ref[:, lanes].astype(jnp.float32)
            ).astype(jnp.bfloat16)
        return fetch(q, gx_ref.at[:, columns(q)], gx_hbm.at[:, columns(q)])

    depth, width = rows.shape[1] * rows.shape[2], rows.shape[3]

    def accumulate(slots):
        for c in range(2):
            at, size = chunks[c]
            total = None
            for slot in slots:
                origin = lax.rem(y + Y_SIZE - slot, Y_SIZE) if slot <= 4 else lax.rem(y + slot - 4, Y_SIZE)
                left = rows[origin].reshape(depth, width)
                right = (hid_ref if slot == 0 else hidden.at[slot])[pl.ds(at, size), :]
                term = lax.dot_general(
                    left, right, (((0,), (1,)), ((), ())), preferred_element_type=jnp.float32
                )
                total = term if total is None else total + term
            total = total.reshape(16, SLOTS, size)
            if 0 in slots:
                partial[:, :, at : at + size] = total
            else:
                partial[:, :, at : at + size] += total

    message[...] = jnp.zeros_like(message)
    for c in small:
        c.wait()
    route(ids_ref, gate_ref, cot_ref, routed_ref)
    prepare(0)
    scan_states_whole(0)
    held_units.wait()
    pl.semaphore_wait(barrier, len(greeted))

    sliced = [
        copy(routed_ref.at[lax.rem(y + k, Y_SIZE)], slices.at[y], ds.at[k], dr.at[k], on_y(k))
        for k in range(1, Y_SIZE)
    ]
    pass_on(0)
    slices[y] = routed_ref[y]
    prepare(1)
    scan_states_whole(1)
    first_told = tell(0)
    for c in sliced:
        c.wait_recv()
    rows[:, j] = slices[...]
    spread = [
        copy(slices, rows.at[:, j], zs.at[k], zr.at[k], on_seq(2 * k)) for k in range(1, 4)
    ]
    spread.append(copy(slices, rows.at[:, j], zs.at[0], zr.at[0], {"dp": i, "seq": sibling}))
    prepare(2)
    carry = scan_states(2, 0, (zero, (zero,) * states))
    pass_on(1)
    finish_states(2, scan_states(2, 1, carry))
    prepare(3)
    scan_states_whole(3)
    second_told = tell(1)
    first_back = combine(0, first_told)
    pass_on(2)
    forwarded = []
    for k in range(1, 4):
        spread[k - 1].wait_recv()
        origin = lax.rem(j + PEERS - 2 * k, PEERS)
        forwarded.append(
            copy(rows.at[:, origin], rows.at[:, origin], fs.at[k], fr.at[k], {"dp": i, "seq": sibling})
        )
    spread[3].wait_recv()
    for c in forwarded:
        c.wait_recv()
    accumulate((0, 1, 5))
    second_back = combine(1, second_told)
    pass_on(3)
    for c in first_back:
        c.wait_recv()
    done = [scan_outputs(0)]
    for c in range(2):
        gathered[2, c, 1].wait_recv()
    accumulate((2, 3, 6, 7))
    for c in range(2):
        gathered[3, c, 0].wait_recv()
    accumulate((4,))
    rounded[...] = partial[...].astype(jnp.bfloat16)
    scattered = []
    for c in range(2):
        at, size = chunks[c]
        for k in range(1, 16):
            other, device = on_plane(k)
            scattered.append(
                copy(
                    rounded.at[other, :, pl.ds(at, size)], parts.at[k, :, pl.ds(at, size)],
                    ps.at[c, k], pr.at[c, k], device,
                )
            )
    done.append(scan_outputs(1))
    for c in second_back:
        c.wait_recv()
    done.append(scan_outputs(2))
    done.append(scan_outputs(3))
    for c in range(2):
        at, size = chunks[c]
        total = partial[zx, :, at : at + size]
        for k in range(1, 16):
            scattered[c * 15 + k - 1].wait_recv()
            total = total + parts[k, :, at : at + size].astype(jnp.float32)
        down_ref[:, at : at + size] = total
    done.append(fetch(4, down_ref, down_hbm))
    for c in started:
        c.wait_send()
    for c in done:
        c.wait()


def fused(out_coef, in_coef, ids, gate, cot, hid, x, w, b, d, g, skip):
    units, depth = hid.shape
    tokens, width = cot.shape
    width = width // Y_SIZE
    channels, states = w.shape[1], d.shape[0]
    quarters, tiles = channels // TILE, TILE // LANES
    sent, lines = 2 * states + 8, 2 * states
    hbm = pl.BlockSpec(memory_space=pl.ANY)
    smem = pl.BlockSpec(memory_space=pltpu.SMEM)
    sem, f32, bf16 = pltpu.SemaphoreType.DMA, jnp.float32, jnp.bfloat16
    arrays = (ids, gate, cot, hid, x, w, b, d, g, skip)
    return pl.pallas_call(
        fused_kernel,
        in_specs=[smem] * 2 + [hbm] * len(arrays),
        out_specs=[hbm] * 2,
        out_shape=[
            jax.ShapeDtypeStruct((SLOTS, units), f32),
            jax.ShapeDtypeStruct((tokens, channels), bf16),
        ],
        scratch_shapes=[pltpu.VMEM(a.shape, a.dtype) for a in arrays] + [
            pltpu.VMEM((SLOTS, units), f32),
            pltpu.VMEM((tokens, channels), bf16),
            pltpu.VMEM((Y_SIZE, SLOTS, width), bf16),
            pltpu.VMEM((quarters, tiles * tokens, LANES), f32),
            pltpu.VMEM((quarters, tiles * tokens, LANES), f32),
            pltpu.VMEM((quarters, tiles * states, LANES), f32),
            pltpu.VMEM((2, PEERS * sent, LANES), f32),
            pltpu.VMEM((2, PEERS, sent, LANES), f32),
            pltpu.VMEM((2, PEERS, lines, LANES), f32),
            pltpu.VMEM((2, PEERS * lines, LANES), f32),
            pltpu.VMEM((tiles * tokens, LANES), f32),
            pltpu.VMEM((8, units, depth), bf16),
            pltpu.VMEM((Y_SIZE, SLOTS, width), bf16),
            pltpu.VMEM((Y_SIZE, PEERS, SLOTS, width), bf16),
            pltpu.VMEM((16, SLOTS, units), f32),
            pltpu.VMEM((16, SLOTS, units), bf16),
            pltpu.VMEM((16, SLOTS, units), bf16),
            sem((16,)),
            sem((2, 8)), sem((2, 8)),
            sem((8,)), sem((8,)),
            sem((4,)), sem((4,)),
            sem((4,)), sem((4,)),
            sem((2, 8)), sem((2, 8)),
            sem((2, 8)), sem((2, 8)),
            sem((2, 16)), sem((2, 16)),
        ],
        compiler_params=pltpu.CompilerParams(
            collective_id=0, has_side_effects=True, vmem_limit_bytes=VMEM_LIMIT
        ),
        name="fused",
    )(out_coef, in_coef, *arrays)


def on_device(
    cotangent, expert_ids, gate_probs, hidden_acts, step_input, step_proj, step_bias,
    decay_rate, input_coef, output_coef, grad_output, skip_weight,
):
    grad_down, grad_x = fused(
        output_coef[0], input_coef[0], expert_ids[0].T, gate_probs[0].T, cotangent[0], hidden_acts,
        step_input[0], step_proj, step_bias[None, :], decay_rate, grad_output[0], skip_weight[None, :],
    )
    return (grad_down, grad_x[None])


def solution(mesh):
    return jax.shard_map(
        on_device,
        mesh=mesh,
        in_specs=(
            P("dp", "seq", None),
            P("dp", "seq", None),
            P("dp", "seq", None),
            P("seq", "dp"),
            P("dp", "seq", None),
            P(),
            P(),
            P(),
            P("dp", None, "seq"),
            P("dp", None, "seq"),
            P("dp", "seq", None),
            P(),
        ),
        out_specs=(P("dp", "seq"), P("dp", "seq", None)),
        check_vma=False,
    )
```

```python
import functools
import math

import jax
import jax.numpy as jnp
from jax import lax
from jax.experimental import pallas as pl
from jax.experimental.pallas import tpu as pltpu
from jax.sharding import PartitionSpec as P

MESH = pl.DeviceIdType.MESH
LANES = 128
TILE = 8 * LANES
LOG2E = math.log2(math.e)
UNROLL = 4
X_SIZE = 8
Y_SIZE = 8
PEERS = 8
SLOTS = 16
VMEM_LIMIT = 56 << 20
PAD = 8


def softplus(v):
    return jnp.maximum(v, 0.0) + jnp.log1p(jnp.exp(-jnp.abs(v)))


def route(ids_ref, gate_ref, cot_ref, routed_ref):
    tokens = cot_ref.shape[0]
    named = (ids_ref[...] == 0).astype(jnp.float32)
    chosen = jnp.sum(named, axis=0, keepdims=True)
    gate = jnp.sum(named * gate_ref[...], axis=0, keepdims=True)
    row = lax.broadcasted_iota(jnp.int32, (tokens, tokens), 0)
    col = lax.broadcasted_iota(jnp.int32, (tokens, tokens), 1)
    earlier = jnp.where(row < col, 1.0, 0.0).astype(jnp.bfloat16)
    spread = jnp.broadcast_to(chosen, (SLOTS, tokens))
    rank = jnp.dot(spread.astype(jnp.bfloat16), earlier, preferred_element_type=jnp.float32)
    slot = lax.broadcasted_iota(jnp.int32, (SLOTS, tokens), 0).astype(jnp.float32)
    pick = jnp.where(rank == slot, spread, 0.0)
    weight = jnp.sum(pick * gate, axis=1, keepdims=True)
    width = routed_ref.shape[2]
    for y in range(routed_ref.shape[0]):
        picked = jnp.dot(
            pick.astype(jnp.bfloat16),
            cot_ref[:, y * width : (y + 1) * width],
            preferred_element_type=jnp.float32,
        )
        routed_ref[y] = (weight * picked).astype(jnp.bfloat16)


def fused_kernel(
    out_coef, in_coef, ids_hbm, gate_hbm, cot_hbm, hid_hbm, x_hbm, w_hbm, b_hbm, d_hbm, g_hbm, skip_hbm,
    down_hbm, gx_hbm,
    ids_ref, gate_ref, cot_ref, hid_ref, x_ref, w_ref, b_ref, d_ref, g_ref, skip_ref, down_ref, gx_ref,
    routed_ref, steps, grads, rates, message, told, sums, arrived, results,
    hidden, slices, rows, partial, rounded, parts,
    local, hs, hr, ds, dr, zs, zr, fs, fr, ss, sr, ts, tr, ps, pr,
):
    i, j = lax.axis_index("dp"), lax.axis_index("seq")
    y, zx = i // 16, lax.rem(i, 16)
    zl, x = zx // 8, lax.rem(zx, 8)
    units = hid_ref.shape[0]
    split = units // 2 // LANES * LANES + LANES
    chunks = ((0, split), (split, units - split))
    sibling = j + 1 - 2 * lax.rem(j, 2)
    tokens, states, tiles = x_ref.shape[0], d_ref.shape[0], TILE // LANES
    quarters = w_ref.shape[1] // TILE
    pairs = quarters // 2
    sent = told.shape[2]
    lines = 2 * states

    def fetch(k, src, dst):
        c = pltpu.make_async_copy(src, dst, local.at[k])
        c.start()
        return c

    def span(k):
        return slice(k * (tokens + PAD), k * (tokens + PAD) + tokens)

    def columns(q):
        return pl.ds(q * TILE, TILE)

    small = [
        fetch(0, ids_hbm, ids_ref), fetch(1, gate_hbm, gate_ref), fetch(2, cot_hbm, cot_ref),
        fetch(3, x_hbm, x_ref), fetch(4, b_hbm, b_ref), fetch(5, d_hbm, d_ref), fetch(6, skip_hbm, skip_ref),
    ]
    weights, outputs = [], []
    for q in range(quarters):
        weights.append(fetch(8 + q, w_hbm.at[:, columns(q)], w_ref.at[:, columns(q)]))
        outputs.append(fetch(12 + q, g_hbm.at[:, columns(q)], g_ref.at[:, columns(q)]))
    held_units = fetch(7, hid_hbm, hid_ref)

    def on_y(k):
        return {"dp": lax.rem(y + k, Y_SIZE) * 16 + zx, "seq": j}

    def on_seq(k):
        return {"dp": i, "seq": lax.rem(j + k, PEERS)}

    def on_plane(k):
        other = lax.rem(zl + k // 8, 2) * 8 + lax.rem(x + k % 8, 8)
        return other, {"dp": y * 16 + other, "seq": j}

    barrier = pltpu.get_barrier_semaphore()
    greeted = [on_y(k) for k in range(1, Y_SIZE)]
    greeted += [on_seq(k) for k in range(1, PEERS)]
    greeted += [on_plane(k)[1] for k in range(1, 16)]
    for device in greeted:
        pl.semaphore_signal(barrier, inc=1, device_id=device, device_id_type=MESH)

    started = []

    def copy(src, dst, send, recv, device):
        c = pltpu.make_async_remote_copy(
            src_ref=src, dst_ref=dst, send_sem=send, recv_sem=recv,
            device_id=device, device_id_type=MESH,
        )
        c.start()
        started.append(c)
        return c

    gathered = {}

    def pass_on(hop):
        for c in range(2):
            at, size = chunks[c]
            here = pl.ds(at, size)
            for way, final in ((0, 4), (1, 3)):
                if hop < final:
                    if hop:
                        gathered[hop - 1, c, way].wait_recv()
                    slot = hop if way == 0 else 4 + hop
                    land = hop + 1 if way == 0 else 5 + hop
                    source = hid_ref if hop == 0 else hidden.at[slot]
                    gathered[hop, c, way] = copy(
                        source.at[here], hidden.at[land, here], hs.at[c, land], hr.at[c, land],
                        on_y(1 if way == 0 else Y_SIZE - 1),
                    )

    def prepare(q):
        weights[q].wait()
        outputs[q].wait()
        own = slice(q * TILE, (q + 1) * TILE)
        step = softplus(
            jnp.dot(x_ref[...], w_ref[:, own], preferred_element_type=jnp.float32) + b_ref[:, own]
        )
        g = g_ref[:, own].astype(jnp.float32)
        d = d_ref[:, own] * (-LOG2E)
        for k in range(tiles):
            lanes = slice(k * LANES, (k + 1) * LANES)
            steps[q, span(k), :] = step[:, lanes]
            grads[q, span(k), :] = g[:, lanes]
            rates[q, k * states : (k + 1) * states, :] = d[:, lanes]

    def rate_of(q):
        return [rates[q, pl.ds(n, tiles, stride=states), :] for n in range(states)]

    def at_token(ref, q, t):
        return ref[q, pl.ds(t, tiles, stride=tokens + PAD), :]

    zero = jnp.zeros((tiles, LANES), jnp.float32)

    def scan_states(q, half, carry):
        rate = rate_of(q)
        count = tokens // 2

        def body(k, carry):
            total, held = carry
            t = tokens - 1 - half * count - k
            s, grad = at_token(steps, q, t), at_token(grads, q, t)
            held = tuple(
                jnp.exp2(s * rate[n]) * (out_coef[n, t] * grad + held[n]) for n in range(states)
            )
            return total + s, held

        return lax.fori_loop(0, count, body, carry, unroll=UNROLL)

    def finish_states(q, carry):
        total, held = carry
        for n in range(states):
            message[q // 2, pl.ds(q % 2 * states + n, tiles, stride=sent), :] = held[n]
        message[q // 2, pl.ds(lines + q % 2, tiles, stride=sent), :] = total

    def scan_states_whole(q):
        finish_states(q, scan_states(q, 1, scan_states(q, 0, (zero, (zero,) * states))))

    def tell(a):
        return [
            copy(
                message.at[a, pl.ds(pl.multiple_of(lax.rem(j + k, PEERS) * sent, 8), sent), :],
                told.at[a, j], ss.at[a, k], sr.at[a, k], on_seq(k),
            )
            for k in range(1, PEERS)
        ]

    def combine(a, incoming):
        told[a, j] = message[a, pl.ds(pl.multiple_of(j * sent, 8), sent), :]
        mine = pl.ds(pl.multiple_of(j * states, 8), states)
        factor = jnp.concatenate([rates[2 * a, mine, :], rates[2 * a + 1, mine, :]], axis=0)
        for c in incoming:
            c.wait_recv()
        current = jnp.zeros((lines, LANES), jnp.float32)
        for b in reversed(range(PEERS)):
            sums[a, b] = current
            if b:
                total = jnp.concatenate(
                    [
                        jnp.broadcast_to(told[a, b, lines + k : lines + k + 1, :], (states, LANES))
                        for k in range(2)
                    ],
                    axis=0,
                )
                current = told[a, b, :lines, :] + jnp.exp2(factor * total) * current
        slot = pl.ds(pl.multiple_of(j * lines, 8), lines)
        back = [
            copy(
                sums.at[a, lax.rem(j + k, PEERS)], arrived.at[a, slot, :], ts.at[a, k], tr.at[a, k], on_seq(k)
            )
            for k in range(1, PEERS)
        ]
        arrived[a, slot, :] = sums[a, j]
        return back

    def scan_outputs(q):
        rate = rate_of(q)

        def body(k, held):
            t = tokens - 1 - k
            s, grad = at_token(steps, q, t), at_token(grads, q, t)
            after, total = [], [None] * 4
            for n in range(states):
                adjoint = out_coef[n, t] * grad + held[n]
                product = in_coef[n, t] * adjoint
                total[n % 4] = product if n < 4 else total[n % 4] + product
                after.append(jnp.exp2(s * rate[n]) * adjoint)
            results[pl.ds(t, tiles, stride=tokens + PAD), :] = s * ((total[0] + total[1]) + (total[2] + total[3]))
            return tuple(after)

        held = tuple(
            arrived[q // 2, pl.ds(q % 2 * states + n, tiles, stride=lines), :] for n in range(states)
        )
        lax.fori_loop(0, tokens, body, held, unroll=UNROLL)
        for k in range(tiles):
            lanes = slice(q * TILE + k * LANES, q * TILE + (k + 1) * LANES)
            gx_ref[:, lanes] = (
                results[span(k), :]
                + skip_ref[:, lanes] * g_ref[:, lanes].astype(jnp.float32)
            ).astype(jnp.bfloat16)
        return fetch(q, gx_ref.at[:, columns(q)], gx_hbm.at[:, columns(q)])

    depth, width = rows.shape[1] * rows.shape[2], rows.shape[3]

    def accumulate(slots, which=(0, 1)):
        for c in which:
            at, size = chunks[c]
            total = None
            for slot in slots:
                origin = lax.rem(y + Y_SIZE - slot, Y_SIZE) if slot <= 4 else lax.rem(y + slot - 4, Y_SIZE)
                left = rows[origin].reshape(depth, width)
                right = (hid_ref if slot == 0 else hidden.at[slot])[pl.ds(at, size), :]
                term = lax.dot_general(
                    left, right, (((0,), (1,)), ((), ())), preferred_element_type=jnp.float32
                )
                total = term if total is None else total + term
            total = total.reshape(16, SLOTS, size)
            if 0 in slots:
                partial[:, :, at : at + size] = total
            else:
                partial[:, :, at : at + size] += total

    message[...] = jnp.zeros_like(message)
    for c in small:
        c.wait()
    route(ids_ref, gate_ref, cot_ref, routed_ref)
    prepare(0)
    scan_states_whole(0)
    held_units.wait()
    pl.semaphore_wait(barrier, len(greeted))

    sliced = [
        copy(routed_ref.at[lax.rem(y + k, Y_SIZE)], slices.at[y], ds.at[k], dr.at[k], on_y(k))
        for k in range(1, Y_SIZE)
    ]
    pass_on(0)
    slices[y] = routed_ref[y]
    prepare(1)
    scan_states_whole(1)
    first_told = tell(0)
    for c in sliced:
        c.wait_recv()
    rows[:, j] = slices[...]
    spread = [
        copy(slices, rows.at[:, j], zs.at[k], zr.at[k], on_seq(2 * k)) for k in range(1, 4)
    ]
    spread.append(copy(slices, rows.at[:, j], zs.at[0], zr.at[0], {"dp": i, "seq": sibling}))
    prepare(2)
    carry = scan_states(2, 0, (zero, (zero,) * states))
    pass_on(1)
    finish_states(2, scan_states(2, 1, carry))
    prepare(3)
    scan_states_whole(3)
    second_told = tell(1)
    first_back = combine(0, first_told)
    pass_on(2)
    forwarded = []
    for k in range(1, 4):
        spread[k - 1].wait_recv()
        origin = lax.rem(j + PEERS - 2 * k, PEERS)
        forwarded.append(
            copy(rows.at[:, origin], rows.at[:, origin], fs.at[k], fr.at[k], {"dp": i, "seq": sibling})
        )
    spread[3].wait_recv()
    for c in forwarded:
        c.wait_recv()
    accumulate((0, 1, 5))
    second_back = combine(1, second_told)
    pass_on(3)
    for c in first_back:
        c.wait_recv()
    done = [scan_outputs(0)]
    for c in range(2):
        gathered[2, c, 1].wait_recv()
    accumulate((2, 3, 6, 7))
    scattered = []
    for c in range(2):
        at, size = chunks[c]
        gathered[3, c, 0].wait_recv()
        accumulate((4,), (c,))
        rounded[:, :, at : at + size] = partial[:, :, at : at + size].astype(jnp.bfloat16)
        for k in range(1, 16):
            other, device = on_plane(k)
            scattered.append(
                copy(
                    rounded.at[other, :, pl.ds(at, size)], parts.at[k, :, pl.ds(at, size)],
                    ps.at[c, k], pr.at[c, k], device,
                )
            )
    done.append(scan_outputs(1))
    for c in second_back:
        c.wait_recv()
    done.append(scan_outputs(2))
    done.append(scan_outputs(3))
    for c in range(2):
        at, size = chunks[c]
        total = partial[zx, :, at : at + size]
        for k in range(1, 16):
            scattered[c * 15 + k - 1].wait_recv()
            total = total + parts[k, :, at : at + size].astype(jnp.float32)
        down_ref[:, at : at + size] = total
    done.append(fetch(4, down_ref, down_hbm))
    for c in started:
        c.wait_send()
    for c in done:
        c.wait()


def fused(out_coef, in_coef, ids, gate, cot, hid, x, w, b, d, g, skip):
    units, depth = hid.shape
    tokens, width = cot.shape
    width = width // Y_SIZE
    channels, states = w.shape[1], d.shape[0]
    quarters, tiles = channels // TILE, TILE // LANES
    sent, lines = 2 * states + 8, 2 * states
    hbm = pl.BlockSpec(memory_space=pl.ANY)
    smem = pl.BlockSpec(memory_space=pltpu.SMEM)
    sem, f32, bf16 = pltpu.SemaphoreType.DMA, jnp.float32, jnp.bfloat16
    arrays = (ids, gate, cot, hid, x, w, b, d, g, skip)
    return pl.pallas_call(
        fused_kernel,
        in_specs=[smem] * 2 + [hbm] * len(arrays),
        out_specs=[hbm] * 2,
        out_shape=[
            jax.ShapeDtypeStruct((SLOTS, units), f32),
            jax.ShapeDtypeStruct((tokens, channels), bf16),
        ],
        scratch_shapes=[pltpu.VMEM(a.shape, a.dtype) for a in arrays] + [
            pltpu.VMEM((SLOTS, units), f32),
            pltpu.VMEM((tokens, channels), bf16),
            pltpu.VMEM((Y_SIZE, SLOTS, width), bf16),
            pltpu.VMEM((quarters, tiles * (tokens + PAD), LANES), f32),
            pltpu.VMEM((quarters, tiles * (tokens + PAD), LANES), f32),
            pltpu.VMEM((quarters, tiles * states, LANES), f32),
            pltpu.VMEM((2, PEERS * sent, LANES), f32),
            pltpu.VMEM((2, PEERS, sent, LANES), f32),
            pltpu.VMEM((2, PEERS, lines, LANES), f32),
            pltpu.VMEM((2, PEERS * lines, LANES), f32),
            pltpu.VMEM((tiles * (tokens + PAD), LANES), f32),
            pltpu.VMEM((8, units, depth), bf16),
            pltpu.VMEM((Y_SIZE, SLOTS, width), bf16),
            pltpu.VMEM((Y_SIZE, PEERS, SLOTS, width), bf16),
            pltpu.VMEM((16, SLOTS, units), f32),
            pltpu.VMEM((16, SLOTS, units), bf16),
            pltpu.VMEM((16, SLOTS, units), bf16),
            sem((16,)),
            sem((2, 8)), sem((2, 8)),
            sem((8,)), sem((8,)),
            sem((4,)), sem((4,)),
            sem((4,)), sem((4,)),
            sem((2, 8)), sem((2, 8)),
            sem((2, 8)), sem((2, 8)),
            sem((2, 16)), sem((2, 16)),
        ],
        compiler_params=pltpu.CompilerParams(
            collective_id=0, has_side_effects=True, vmem_limit_bytes=VMEM_LIMIT
        ),
        name="fused",
    )(out_coef, in_coef, *arrays)


def on_device(
    cotangent, expert_ids, gate_probs, hidden_acts, step_input, step_proj, step_bias,
    decay_rate, input_coef, output_coef, grad_output, skip_weight,
):
    grad_down, grad_x = fused(
        output_coef[0], input_coef[0], expert_ids[0].T, gate_probs[0].T, cotangent[0], hidden_acts,
        step_input[0], step_proj, step_bias[None, :], decay_rate, grad_output[0], skip_weight[None, :],
    )
    return (grad_down, grad_x[None])


def solution(mesh):
    return jax.shard_map(
        on_device,
        mesh=mesh,
        in_specs=(
            P("dp", "seq", None),
            P("dp", "seq", None),
            P("dp", "seq", None),
            P("seq", "dp"),
            P("dp", "seq", None),
            P(),
            P(),
            P(),
            P("dp", None, "seq"),
            P("dp", None, "seq"),
            P("dp", "seq", None),
            P(),
        ),
        out_specs=(P("dp", "seq"), P("dp", "seq", None)),
        check_vma=False,
    )
```
